32 devices in a mesh: grp: 4 (over x, core), tp: 8 (over z, y).
Axes of the slice: x: 2, y: 2, z: 4, core: 2. Of those that a mesh axis runs over, the one named last changes fastest.
Arguments:
- tokens: bfloat16 [3072, 8192], P(('grp', 'tp')), may hold values from -6 to 6
- holder: int32 [3072, 1], P(('grp', 'tp')), may hold values from 0 to 31; in each aligned block of 96 rows (0 to 95, 96 to 191, ...) at most 6 rows name the same one
- adapter_choice_index: int32 [3072, 1], P(('grp', 'tp')), may hold values from 0 to 1
- query_base_output: bfloat16 [8192, 8192], P(None, 'tp'), may hold values from -0.0625 to 0.0625
- value_base_output: bfloat16 [8192, 1024], P(None, 'tp'), may hold values from -0.0625 to 0.0625
- adapter_down_weight: bfloat16 [64, 8192, 128], P(('grp', 'tp')), may hold values from -0.0625 to 0.0625
- adapter_query_up: bfloat16 [64, 64, 8192], P(('grp', 'tp')), may hold values from -0.75 to 0.75
- adapter_value_up: bfloat16 [64, 64, 1024], P(('grp', 'tp')), may hold values from -0.75 to 0.75
Outputs:
- queries: bfloat16 [3072, 8192], P(('grp', 'tp'))
- values: bfloat16 [3072, 1024], P(('grp', 'tp'))
The draws below stay inside these ranges and needn't reach their ends.
Inputs may be any that keep to these rules, and one draw needn't show every extreme that they name: Among the 96 requests of one device no holder appears more than 6 times, and some holder appears exactly 6 times.
All inputs are finite; a program needn't handle non-finite values.
Results may differ from the reference program's by a relative error of at most 0.0057.
Values may be sent and summed in bfloat16 or wider, within the bound.
A program may use at most 128 MiB of HBM per device.

```python
import math
import jax
import jax.numpy as jnp
import numpy as np
from jax import lax

MODEL_WIDTH = 8192
DQ = 8192
DV = 1024
ADAPTER_RANK = 64
TEN_DEV = 2
TOK_DEV = 96
CAP = 6
ROWS = 3072
ADAPTER_TOTAL = 64
N_GRP = 4
N_TP = 8


def set_ends(result, own_key, least, high):
    longest = result.shape.index(max(result.shape))
    spots = []
    for shift in (0, 1):
        where = [jax.random.randint(jax.random.fold_in(own_key, axis), (), 0, length) for axis, length in enumerate(result.shape)]
        where[longest] = (where[longest] + shift) % result.shape[longest]
        spots.append(tuple(where))
    return result.at[spots[0]].set(least).at[spots[1]].set(high)


def steps_of(stream_key, dims, pieces, low, top_value):
    def one(dim, shards_of):
        steps = jax.random.uniform(jax.random.fold_in(jax.random.fold_in(stream_key, 6), dim), (shards_of,), jnp.float32, low / len(pieces), top_value / len(pieces))
        return jnp.repeat(jnp.exp(steps), dims[dim] // shards_of).reshape((-1,) + (1,) * (len(dims) - dim - 1))

    factor_of = one(*pieces[0])
    for cut in pieces[1:]:
        factor_of = factor_of * one(*cut)
    return factor_of


def shared_out(rng, own, number, rows, number_of, top, most, slope):
    sequence = jax.random.permutation(rng, number_of)
    heavy_load, usual = shares(number_of, rows * top, most, slope, True), shares(number_of, rows * top, most, slope, False)
    places = jnp.arange(number_of)

    def named(lengths, offset_by):
        used = int((lengths > 0).sum())
        fixed = max(1, used // 4)
        shifted = fixed + (places - fixed + offset_by * (used - fixed)) % max(1, number_of - fixed)
        return jnp.zeros((number_of,), jnp.int32).at[sequence[jnp.where(places < fixed, places, shifted)]].set(jnp.asarray(lengths, jnp.int32))

    lengths = jnp.where(number % 4 == 0, named(heavy_load, number // 4), named(usual, number - number // 4 - 1))
    mixed = jax.random.permutation(jax.random.fold_in(own, 3), number_of)
    giver, sink = mixed[0:number_of // 2 * 2:2], mixed[1:number_of // 2 * 2:2]
    margin = jnp.minimum(lengths[giver] - 1, most - lengths[sink]) // 2
    margin = jnp.where((giver == sequence[0]) | (sink == sequence[0]) | (lengths[sink] == 0), 0, jnp.maximum(margin, 0))
    shifted = jax.random.randint(jax.random.fold_in(own, 4), (number_of // 2,), 0, 1 << 20) % (margin + 1)
    lengths = lengths.at[giver].add(-shifted).at[sink].add(shifted)
    labels = jnp.searchsorted(jnp.cumsum(lengths), jnp.arange(rows * top), side="right").astype(jnp.int32)
    table = labels.reshape(top, rows).T
    table = table[jax.random.permutation(jax.random.fold_in(own, 1), rows)]
    offset_by = jax.random.randint(jax.random.fold_in(own, 2), (rows, 1), 0, top)
    return jnp.take_along_axis(table, (jnp.arange(top)[None, :] + offset_by) % top, axis=1)


def shares(count, total, bound, skew, full):
    weights = [(1 << 20) // math.isqrt(standing ** skew) + 1 for standing in range(1, count + 1)]
    largest = bound if full else min(bound, max(-(-total // count), total * weights[0] // sum(weights)))
    least = 1 if total - largest >= count - 1 else 0
    counts, surplus = [largest] + [least] * (count - 1), total - largest - least * (count - 1)
    while surplus > 0:
        candidates = [i for i in range(1, count) if counts[i] < largest] or [i for i in range(1, count) if counts[i] < bound]
        mass, budget = sum([weights[i] for i in candidates]), surplus
        for i in candidates:
            addition = min(bound - counts[i], max(1, budget * weights[i] // mass), surplus)
            counts[i] = counts[i] + addition
            surplus = surplus - addition
    return np.array(counts)


def scatter_about(rng, shape, width, bound, shards=(), dtype=jnp.bfloat16):
    result = width * jax.random.normal(rng, shape, jnp.float32)
    if shards:
        result = result * steps_of(rng, shape, shards, -0.22, 0.18)
    return jnp.clip(result, -bound, bound).astype(dtype)


def setup_inputs(seed: int = 0) -> dict:
    seeds = jax.random.split(jax.random.key(seed), 9)
    tokens = scatter_about(seeds[0], (ROWS, MODEL_WIDTH), 1.0, 6.0, ((0, 32),))
    holder_keys = jax.random.split(jax.random.fold_in(seeds[1], 1), ROWS // TOK_DEV)
    holder_turns = jax.random.permutation(jax.random.fold_in(seeds[1], 3), ROWS // TOK_DEV)
    holder = jax.vmap(lambda own, number: shared_out(jax.random.fold_in(seeds[1], 2), own, number, TOK_DEV, N_GRP * N_TP, 1, CAP, 2))(holder_keys, holder_turns).reshape((ROWS, 1))
    adapter_choice_index = set_ends(jax.random.randint(seeds[2], (ROWS, 1), 0, TEN_DEV), jax.random.fold_in(seeds[2], 1), 0, TEN_DEV - 1).astype(jnp.int32)
    query_base_output = scatter_about(seeds[3], (MODEL_WIDTH, DQ), MODEL_WIDTH ** -0.5, 0.0625, ((1, 8),))
    value_base_output = scatter_about(seeds[4], (MODEL_WIDTH, DV), MODEL_WIDTH ** -0.5, 0.0625, ((1, 8),))
    adapter_down_weight = scatter_about(seeds[5], (ADAPTER_TOTAL, MODEL_WIDTH, 2 * ADAPTER_RANK), MODEL_WIDTH ** -0.5, 0.0625, ((0, 32),))
    adapter_query_up = scatter_about(seeds[6], (ADAPTER_TOTAL, ADAPTER_RANK, DQ), ADAPTER_RANK ** -0.5, 0.75, ((0, 32),))
    adapter_value_up = scatter_about(seeds[7], (ADAPTER_TOTAL, ADAPTER_RANK, DV), ADAPTER_RANK ** -0.5, 0.75, ((0, 32),))
    return dict(tokens=tokens, holder=holder, adapter_choice_index=adapter_choice_index, query_base_output=query_base_output, value_base_output=value_base_output, adapter_down_weight=adapter_down_weight, adapter_query_up=adapter_query_up, adapter_value_up=adapter_value_up)


adapter_scale = 2.0


def reference(tokens, holder, adapter_choice_index, query_base_output, value_base_output, adapter_down_weight, adapter_query_up, adapter_value_up):
    tenant = (holder[:, 0] * TEN_DEV + adapter_choice_index[:, 0]).astype(jnp.int32)
    plain_query = jnp.dot(tokens, query_base_output, preferred_element_type=jnp.float32).astype(jnp.bfloat16)
    plain_value = jnp.dot(tokens, value_base_output, preferred_element_type=jnp.float32).astype(jnp.bfloat16)
    block_rows = 8
    row_blocks = tokens.reshape(ROWS // block_rows, block_rows, MODEL_WIDTH)
    tenant_blocks = tenant.reshape(ROWS // block_rows, block_rows)

    def one_block(pair):
        rows, adapter_index = pair
        down_weight = adapter_down_weight[adapter_index].astype(jnp.float32)
        reduced_state = jnp.einsum("bd,bdk->bk", rows.astype(jnp.float32), down_weight).astype(jnp.bfloat16)
        query_up_weight = adapter_query_up[adapter_index].astype(jnp.float32)
        value_up_weight = adapter_value_up[adapter_index].astype(jnp.float32)
        query_correction = (adapter_scale * jnp.einsum("jt,jtd->jd", reduced_state[:, :ADAPTER_RANK].astype(jnp.float32), query_up_weight)).astype(jnp.bfloat16)
        value_correction = (adapter_scale * jnp.einsum("jt,jtd->jd", reduced_state[:, ADAPTER_RANK:].astype(jnp.float32), value_up_weight)).astype(jnp.bfloat16)
        return query_correction, value_correction

    query_correction, value_correction = lax.map(one_block, (row_blocks, tenant_blocks))
    query_correction = query_correction.reshape(ROWS, DQ)
    value_correction = value_correction.reshape(ROWS, DV)
    queries = (plain_query.astype(jnp.float32) + query_correction.astype(jnp.float32)).astype(jnp.bfloat16)
    values = (plain_value.astype(jnp.float32) + value_correction.astype(jnp.float32)).astype(jnp.bfloat16)
    return queries, values
```

```python
import jax
import jax.numpy as jnp
from jax import lax
from jax.sharding import PartitionSpec as P

adapter_scale = 2.0
F32 = jnp.float32
BF16 = jnp.bfloat16


def up_term(low, tenant, up):
    count, rank, cols = up.shape
    ids = jnp.arange(count, dtype=jnp.int32)
    flat = up.reshape(count * rank, cols)

    def rows_of(part):
        rows_low, rows_tenant = part
        wide = jnp.where(
            (rows_tenant[:, None] == ids[None, :])[:, :, None], rows_low[:, None, :], jnp.zeros((), BF16)
        )
        return jnp.dot(wide.reshape(rows_low.shape[0], count * rank), flat, preferred_element_type=F32)

    rows = low.shape[0]
    pieces = max(1, (rows * count * rank) // (1 << 22))
    if pieces == 1:
        return rows_of((low, tenant))
    out = lax.map(rows_of, (low.reshape(pieces, rows // pieces, rank), tenant.reshape(pieces, rows // pieces)))
    return out.reshape(rows, cols)


def on_device(tokens, holder, choice, wq, wv, down, up_q, up_v):
    members = lax.axis_size("tp")
    groups = lax.axis_size("grp")
    each = down.shape[0]
    rank = up_q.shape[1]
    tenant = (holder[:, 0] * each + choice[:, 0]).astype(jnp.int32)
    tenant = lax.all_gather(tenant, "tp", axis=0, tiled=True)
    piece = lax.all_gather(tokens, "tp", axis=0, tiled=True)
    downs = lax.all_gather(down, "grp", axis=0, tiled=True)
    all_q = lax.all_to_all(up_q, "tp", split_axis=2, concat_axis=0, tiled=True)
    all_v = lax.all_to_all(up_v, "tp", split_axis=2, concat_axis=0, tiled=True)
    all_q = lax.all_gather(all_q, "grp", axis=0, tiled=True)
    all_v = lax.all_gather(all_v, "grp", axis=0, tiled=True)

    slot = jnp.arange(groups * each, dtype=jnp.int32)
    here = ((slot // each) * members + lax.axis_index("tp")) * each + slot % each
    low = jnp.zeros((piece.shape[0], down.shape[2]), F32)
    for a in range(groups * each):
        part = jnp.dot(piece, downs[a], preferred_element_type=F32)
        low = low + jnp.where((tenant == here[a])[:, None], part, 0.0)
    low = lax.psum(low.astype(BF16), "tp")
    low = (adapter_scale * low).astype(BF16)

    base_q = jnp.dot(piece, wq, preferred_element_type=F32)
    base_v = jnp.dot(piece, wv, preferred_element_type=F32)
    out_q = (base_q + up_term(low[:, :rank], tenant, all_q)).astype(BF16)
    out_v = (base_v + up_term(low[:, rank:], tenant, all_v)).astype(BF16)
    queries = lax.all_to_all(out_q, "tp", split_axis=0, concat_axis=1, tiled=True)
    values = lax.all_to_all(out_v, "tp", split_axis=0, concat_axis=1, tiled=True)
    return queries, values


def solution(mesh):
    rows = P(("grp", "tp"), None)
    blocks = P(("grp", "tp"), None, None)
    return jax.shard_map(
        on_device,
        mesh=mesh,
        in_specs=(rows, rows, rows, P(None, "tp"), P(None, "tp"), blocks, blocks, blocks),
        out_specs=(rows, rows),
        check_vma=False,
    )
```

```python
import functools

import jax
import jax.numpy as jnp
from jax import lax
from jax.experimental import pallas as pl
from jax.experimental.pallas import tpu as pltpu
from jax.sharding import PartitionSpec as P

adapter_scale = 2.0
F32 = jnp.float32
BF16 = jnp.bfloat16
MESH = pl.DeviceIdType.MESH


def factor(n):
    first = 1
    while first * first < n:
        first *= 2
    return first, n // first


class Chain:
    def __init__(self, n1, n2, a, b, place, own, send, recv, device):
        self.n1, self.n2, self.a, self.b = n1, n2, a, b
        self.place, self.own, self.send, self.recv, self.device = place, own, send, recv, device

    def copy(self, block, s, t, way, to_a, to_b):
        return pltpu.make_async_remote_copy(
            src_ref=block,
            dst_ref=self.place(s, t),
            send_sem=self.send.at[s, t, way],
            recv_sem=self.recv.at[s, t],
            device_id=self.device(to_a, to_b),
            device_id_type=MESH,
        )

    def ways(self, s, t):
        a, b = self.a, self.b
        in_line = t == b
        return (
            (in_line & (s <= a) & (a + 1 < self.n1), 0, a + 1, b),
            (in_line & (s >= a) & (a >= 1), 1, a - 1, b),
            ((t <= b) & (b + 1 < self.n2), 2, a, b + 1),
            ((t >= b) & (b >= 1), 3, a, b - 1),
        )

    def each(self, s, t, act, own):
        block = self.own if own else self.place(s, t)
        for cond, way, to_a, to_b in self.ways(s, t):
            if self.n2 == 1 and way >= 2:
                continue

            @pl.when(cond)
            def _(way=way, to_a=to_a, to_b=to_b):
                act(self.copy(block, s, t, way, to_a, to_b))

    def begin(self):
        self.each(self.a, self.b, lambda c: c.start(), True)

    def arrive(self, s, t):
        self.copy(self.place(s, t), s, t, 0, self.a, self.b).wait_recv()
        self.each(s, t, lambda c: c.start(), False)

    def first_step(self, d):
        for s, ok in ((self.a - d, self.a >= d), (self.a + d, self.a + d < self.n1)):

            @pl.when(ok)
            def _(s=s):
                self.arrive(s, self.b)

    def second_step(self, d, e):
        sides = ((self.a, None),) if d == 0 else ((self.a - d, self.a >= d), (self.a + d, self.a + d < self.n1))
        for s, ok in sides:
            for t, ok2 in ((self.b - e, self.b >= e), (self.b + e, self.b + e < self.n2)):

                @pl.when(ok2 if ok is None else ok & ok2)
                def _(s=s, t=t):
                    self.arrive(s, t)

    def finish_second(self):
        for d in range(self.n1):
            for e in range(1, self.n2):
                self.second_step(d, e)

    def drain(self):
        def body(i, carry):
            s, t = i // self.n2, i % self.n2
            self.each(s, t, lambda c: c.wait_send(), False)
            return carry

        lax.fori_loop(0, self.n1 * self.n2, body, 0)


def exchange(
    sizes, tok, ten, down, upq, upv,
    tok_all, ten_all, down_all, upq_all, upv_all,
    tok_buf, ten_buf, down_buf, upq_buf, upv_buf,
    big_s, big_r, small_s, small_r, down_s, down_r, q_s, q_r, v_s, v_r,
    pq_s, pq_r, pv_s, pv_r, pt_s, pt_r, local_in, local_out,
):
    groups, members = sizes
    n1, n2 = factor(members)
    nx, nc = groups // 2, 2
    grp, tp = lax.axis_index("grp"), lax.axis_index("tp")
    a, b = tp // n2, tp % n2
    gx, gc = grp // nc, grp % nc
    rows = tok.shape[0]
    cols_q = upq.shape[2] // members
    cut = (rows // (members - 2) // 16 * 16) or 16

    barrier = pltpu.get_barrier_semaphore()
    for i in range(1, members):
        pl.semaphore_signal(barrier, inc=1, device_id=(grp, lax.rem(tp + i, members)), device_id_type=MESH)
    for i in range(1, groups):
        pl.semaphore_signal(barrier, inc=1, device_id=(lax.rem(grp + i, groups), tp), device_id_type=MESH)
    pl.semaphore_wait(barrier, members + groups - 2)

    def at_tp(first, second):
        return (grp, first * n2 + second)

    def at_tp_swapped(second, first):
        return (grp, first * n2 + second)

    def at_grp(first, second):
        return (first * nc + second, tp)

    big = Chain(
        n1, n2, a, b, lambda s, t: tok_all.at[s * n2 + t, pl.ds(cut, rows - cut)],
        tok.at[pl.ds(cut, rows - cut)], big_s, big_r, at_tp,
    )
    small = Chain(
        n2, n1, b, a, lambda t, s: tok_all.at[s * n2 + t, pl.ds(0, cut)],
        tok.at[pl.ds(0, cut)], small_s, small_r, at_tp_swapped,
    )
    downs = Chain(nx, nc, gx, gc, lambda s, t: down_all.at[s * nc + t], down, down_s, down_r, at_grp)
    ups_q = Chain(
        nx, nc, gx, gc, lambda s, t: upq_all.at[s * nc + t], upq_all.at[grp], q_s, q_r, at_grp
    )
    ups_v = Chain(
        nx, nc, gx, gc, lambda s, t: upv_all.at[s * nc + t], upv_all.at[grp], v_s, v_r, at_grp
    )

    def columns(ref, width, j):
        return ref.at[:, :, pl.ds(pl.multiple_of(j * width, width), width)]

    def peers(j, src_tp):
        dev = (grp, j)
        return (
            pltpu.make_async_remote_copy(
                src_ref=columns(upq, cols_q, j), dst_ref=upq_all.at[grp, src_tp],
                send_sem=pq_s.at[j], recv_sem=pq_r.at[src_tp], device_id=dev, device_id_type=MESH),
            pltpu.make_async_remote_copy(
                src_ref=upv.at[j], dst_ref=upv_all.at[grp, src_tp],
                send_sem=pv_s.at[j], recv_sem=pv_r.at[src_tp], device_id=dev, device_id_type=MESH),
            pltpu.make_async_remote_copy(
                src_ref=ten, dst_ref=ten_all.at[src_tp],
                send_sem=pt_s.at[j], recv_sem=pt_r.at[src_tp], device_id=dev, device_id_type=MESH),
        )

    small.begin()
    big.begin()
    downs.begin()
    for i in range(1, members):
        for copy in peers(lax.rem(tp + i, members), tp):
            copy.start()

    moves = (
        (columns(upq, cols_q, tp), upq_buf, upq_all.at[grp, tp]),
        (upv.at[tp], upv_buf, upv_all.at[grp, tp]),
        (ten, ten_buf, ten_all.at[tp]),
        (tok, tok_buf, tok_all.at[tp]),
        (down, down_buf, down_all.at[grp]),
    )
    for i, (source, held, target) in enumerate(moves):
        pltpu.make_async_copy(source, held, local_in.at[i]).start()
    for i, (source, held, target) in enumerate(moves):
        pltpu.make_async_copy(source, held, local_in.at[i]).wait()
        pltpu.make_async_copy(held, target, local_out.at[i]).start()
    for i, (source, held, target) in enumerate(moves):
        pltpu.make_async_copy(held, target, local_out.at[i]).wait()

    for d in range(1, max(n1, n2) + 1):
        if d < n1:
            big.first_step(d)
        if d == 1:
            for e in range(1, n2):
                small.first_step(e)
            for i in range(1, members):
                src_tp = lax.rem(tp + i, members)
                for copy in peers(src_tp, src_tp):
                    copy.wait_recv()
            ups_q.begin()
            ups_v.begin()
        if 1 < d <= n1:
            for e in range(n2):
                small.second_step(e, d - 1)
    for chain in (downs, ups_q, ups_v):
        for d in range(1, nx):
            chain.first_step(d)
    big.finish_second()
    for chain in (downs, ups_q, ups_v):
        chain.finish_second()
    for chain in (big, small, downs, ups_q, ups_v):
        chain.drain()
    for i in range(1, members):
        for copy in peers(lax.rem(tp + i, members), tp):
            copy.wait_send()


def gather_all(tokens, tenant, down, up_q, up_v, groups, members):
    n1, n2 = factor(members)
    nx, nc = groups // 2, 2
    rows = tokens.shape[0]
    each, rank = up_q.shape[:2]
    cq, cv = up_q.shape[2] // members, up_v.shape[2] // members
    ten = jnp.broadcast_to(tenant[:, None], (rows, 128))
    up_v = up_v.reshape(each, rank, members, cv).transpose(2, 0, 1, 3)
    shape = jax.ShapeDtypeStruct
    dma = pltpu.SemaphoreType.DMA
    grid2 = (dma((nx, nc, 4)), dma((nx, nc)))
    return pl.pallas_call(
        functools.partial(exchange, (groups, members)),
        out_shape=(
            shape((members,) + tokens.shape, BF16),
            shape((members, rows, 128), jnp.int32),
            shape((groups,) + down.shape, BF16),
            shape((groups, members, each, rank, cq), BF16),
            shape((groups, members, each, rank, cv), BF16),
        ),
        in_specs=[pl.BlockSpec(memory_space=pl.ANY)] * 5,
        out_specs=(pl.BlockSpec(memory_space=pl.ANY),) * 5,
        scratch_shapes=[
            pltpu.VMEM(tokens.shape, BF16),
            pltpu.VMEM((rows, 128), jnp.int32),
            pltpu.VMEM(down.shape, BF16),
            pltpu.VMEM((each, rank, cq), BF16),
            pltpu.VMEM((each, rank, cv), BF16),
            dma((n1, n2, 4)), dma((n1, n2)),
            dma((n2, n1, 4)), dma((n2, n1)),
            *grid2, *grid2, *grid2,
            dma((members,)), dma((members,)), dma((members,)), dma((members,)), dma((members,)), dma((members,)),
            dma((5,)), dma((5,)),
        ],
        compiler_params=pltpu.CompilerParams(collective_id=0, has_side_effects=True),
    )(tokens, ten, down, up_q, up_v)


def down_kernel(members, tok, ten, down, out):
    step = pl.program_id(0)
    each = down.shape[1]

    @pl.when(step == 0)
    def _():
        out[...] = jnp.zeros_like(out)

    maps = jnp.concatenate([down[0, i] for i in range(each)], axis=1)
    part = jnp.dot(tok[...], maps, preferred_element_type=F32)
    width = down.shape[3]
    first = (step * members + lax.axis_index("tp")) * each
    for i in range(each):
        keep = ten[...] == first + i
        out[...] += jnp.where(keep, part[:, i * width:(i + 1) * width], 0.0).astype(out.dtype)


def down_project(tok, ten, down, members):
    total = tok.shape[0]
    groups = down.shape[0]
    return pl.pallas_call(
        functools.partial(down_kernel, members),
        grid=(groups,),
        out_shape=jax.ShapeDtypeStruct((total, down.shape[3]), BF16),
        in_specs=[
            pl.BlockSpec(tok.shape, lambda g: (0, 0), pipeline_mode=pl.Buffered(1)),
            pl.BlockSpec(ten.shape, lambda g: (0, 0)),
            pl.BlockSpec((1,) + down.shape[1:], lambda g: (g, 0, 0, 0)),
        ],
        out_specs=pl.BlockSpec((total, down.shape[3]), lambda g: (0, 0)),
        compiler_params=pltpu.CompilerParams(vmem_limit_bytes=60 << 20),
    )(tok, ten, down)


def up_term(low, tenant, up):
    count, rank, cols = up.shape
    ids = jnp.arange(count, dtype=jnp.int32)
    flat = up.reshape(count * rank, cols)

    def rows_of(part):
        rows_low, rows_tenant = part
        wide = jnp.where(
            (rows_tenant[:, None] == ids[None, :])[:, :, None], rows_low[:, None, :], jnp.zeros((), BF16)
        )
        return jnp.dot(wide.reshape(rows_low.shape[0], count * rank), flat, preferred_element_type=F32)

    rows = low.shape[0]
    pieces = max(1, (rows * count * rank) // (1 << 22))
    if pieces == 1:
        return rows_of((low, tenant))
    out = lax.map(rows_of, (low.reshape(pieces, rows // pieces, rank), tenant.reshape(pieces, rows // pieces)))
    return out.reshape(rows, cols)


def on_device(tokens, holder, choice, wq, wv, down, up_q, up_v):
    members = lax.axis_size("tp")
    groups = lax.axis_size("grp")
    each, rank, _ = up_q.shape
    mine = (holder[:, 0] * each + choice[:, 0]).astype(jnp.int32)
    tok, ten, downs, all_q, all_v = gather_all(tokens, mine, down, up_q, up_v, groups, members)
    total = members * tokens.shape[0]
    tok = tok.reshape(total, tokens.shape[1])
    ten = ten.reshape(total, 128)
    tenant = ten[:, 0]
    low = down_project(tok, ten, downs, members)
    low = lax.psum(low, "tp")
    low = (adapter_scale * low).astype(BF16)
    base_q = jnp.dot(tok, wq, preferred_element_type=F32)
    base_v = jnp.dot(tok, wv, preferred_element_type=F32)
    count = groups * members * each
    out_q = (base_q + up_term(low[:, :rank], tenant, all_q.reshape(count, rank, -1))).astype(BF16)
    out_v = (base_v + up_term(low[:, rank:], tenant, all_v.reshape(count, rank, -1))).astype(BF16)
    queries = lax.all_to_all(out_q, "tp", split_axis=0, concat_axis=1, tiled=True)
    values = lax.all_to_all(out_v, "tp", split_axis=0, concat_axis=1, tiled=True)
    return queries, values


def solution(mesh):
    rows = P(("grp", "tp"), None)
    blocks = P(("grp", "tp"), None, None)
    return jax.shard_map(
        on_device,
        mesh=mesh,
        in_specs=(rows, rows, rows, P(None, "tp"), P(None, "tp"), blocks, blocks, blocks),
        out_specs=(rows, rows),
        check_vma=False,
    )
```

```python
import functools

import jax
import jax.numpy as jnp
from jax import lax
from jax.experimental import pallas as pl
from jax.experimental.pallas import tpu as pltpu
from jax.sharding import PartitionSpec as P

adapter_scale = 2.0
F32 = jnp.float32
BF16 = jnp.bfloat16
MESH = pl.DeviceIdType.MESH


def factor(n):
    first = 1
    while first * first < n:
        first *= 2
    return first, n // first


class Chain:
    def __init__(self, n1, n2, a, b, place, own, send, recv, device):
        self.n1, self.n2, self.a, self.b = n1, n2, a, b
        self.place, self.own, self.send, self.recv, self.device = place, own, send, recv, device

    def copy(self, block, s, t, way, to_a, to_b):
        return pltpu.make_async_remote_copy(
            src_ref=block,
            dst_ref=self.place(s, t),
            send_sem=self.send.at[s, t, way],
            recv_sem=self.recv.at[s, t],
            device_id=self.device(to_a, to_b),
            device_id_type=MESH,
        )

    def ways(self, s, t):
        a, b = self.a, self.b
        in_line = t == b
        return (
            (in_line & (s <= a) & (a + 1 < self.n1), 0, a + 1, b),
            (in_line & (s >= a) & (a >= 1), 1, a - 1, b),
            ((t <= b) & (b + 1 < self.n2), 2, a, b + 1),
            ((t >= b) & (b >= 1), 3, a, b - 1),
        )

    def each(self, s, t, act, own):
        block = self.own if own else self.place(s, t)
        for cond, way, to_a, to_b in self.ways(s, t):
            if self.n2 == 1 and way >= 2:
                continue

            @pl.when(cond)
            def _(way=way, to_a=to_a, to_b=to_b):
                act(self.copy(block, s, t, way, to_a, to_b))

    def begin(self):
        self.each(self.a, self.b, lambda c: c.start(), True)

    def arrive(self, s, t):
        self.copy(self.place(s, t), s, t, 0, self.a, self.b).wait_recv()
        self.each(s, t, lambda c: c.start(), False)

    def first_step(self, d):
        for s, ok in ((self.a - d, self.a >= d), (self.a + d, self.a + d < self.n1)):

            @pl.when(ok)
            def _(s=s):
                self.arrive(s, self.b)

    def second_step(self, d, e):
        sides = ((self.a, None),) if d == 0 else ((self.a - d, self.a >= d), (self.a + d, self.a + d < self.n1))
        for s, ok in sides:
            for t, ok2 in ((self.b - e, self.b >= e), (self.b + e, self.b + e < self.n2)):

                @pl.when(ok2 if ok is None else ok & ok2)
                def _(s=s, t=t):
                    self.arrive(s, t)

    def finish_second(self):
        for d in range(self.n1):
            for e in range(1, self.n2):
                self.second_step(d, e)

    def drain(self):
        def body(i, carry):
            s, t = i // self.n2, i % self.n2
            self.each(s, t, lambda c: c.wait_send(), False)
            return carry

        lax.fori_loop(0, self.n1 * self.n2, body, 0)


def exchange(
    sizes, tok, ten, down, upq, upv,
    tok_all, ten_all, down_all, upq_all, upv_all,
    tok_buf, ten_buf, down_buf, upq_buf, upv_buf,
    big_s, big_r, small_s, small_r, down_s, down_r, q_s, q_r, v_s, v_r,
    pq_s, pq_r, pv_s, pv_r, pt_s, pt_r, local_in, local_out,
):
    groups, members = sizes
    n1, n2 = factor(members)
    nx, nc = groups // 2, 2
    grp, tp = lax.axis_index("grp"), lax.axis_index("tp")
    a, b = tp // n2, tp % n2
    gx, gc = grp // nc, grp % nc
    rows = tok.shape[0]
    cols_q = upq.shape[2] // members
    cut = (rows // (members - 2) // 16 * 16) or 16

    barrier = pltpu.get_barrier_semaphore()
    for i in range(1, members):
        pl.semaphore_signal(barrier, inc=1, device_id=(grp, lax.rem(tp + i, members)), device_id_type=MESH)
    for i in range(1, groups):
        pl.semaphore_signal(barrier, inc=1, device_id=(lax.rem(grp + i, groups), tp), device_id_type=MESH)
    pl.semaphore_wait(barrier, members + groups - 2)

    def at_tp(first, second):
        return (grp, first * n2 + second)

    def at_tp_swapped(second, first):
        return (grp, first * n2 + second)

    def at_grp(first, second):
        return (first * nc + second, tp)

    big = Chain(
        n1, n2, a, b, lambda s, t: tok_all.at[s * n2 + t, pl.ds(cut, rows - cut)],
        tok.at[pl.ds(cut, rows - cut)], big_s, big_r, at_tp,
    )
    small = Chain(
        n2, n1, b, a, lambda t, s: tok_all.at[s * n2 + t, pl.ds(0, cut)],
        tok.at[pl.ds(0, cut)], small_s, small_r, at_tp_swapped,
    )
    downs = Chain(nx, nc, gx, gc, lambda s, t: down_all.at[s * nc + t], down, down_s, down_r, at_grp)
    ups_q = Chain(
        nx, nc, gx, gc, lambda s, t: upq_all.at[s * nc + t], upq_all.at[grp], q_s, q_r, at_grp
    )
    ups_v = Chain(
        nx, nc, gx, gc, lambda s, t: upv_all.at[s * nc + t], upv_all.at[grp], v_s, v_r, at_grp
    )

    def columns(ref, width, j):
        return ref.at[:, :, pl.ds(pl.multiple_of(j * width, width), width)]

    def peers(j, src_tp):
        dev = (grp, j)
        return (
            pltpu.make_async_remote_copy(
                src_ref=columns(upq, cols_q, j), dst_ref=upq_all.at[grp, src_tp],
                send_sem=pq_s.at[j], recv_sem=pq_r.at[src_tp], device_id=dev, device_id_type=MESH),
            pltpu.make_async_remote_copy(
                src_ref=upv.at[j], dst_ref=upv_all.at[grp, src_tp],
                send_sem=pv_s.at[j], recv_sem=pv_r.at[src_tp], device_id=dev, device_id_type=MESH),
            pltpu.make_async_remote_copy(
                src_ref=ten, dst_ref=ten_all.at[src_tp],
                send_sem=pt_s.at[j], recv_sem=pt_r.at[src_tp], device_id=dev, device_id_type=MESH),
        )

    small.begin()
    big.begin()
    downs.begin()
    for i in range(1, members):
        for copy in peers(lax.rem(tp + i, members), tp):
            copy.start()

    moves = (
        (columns(upq, cols_q, tp), upq_buf, upq_all.at[grp, tp]),
        (upv.at[tp], upv_buf, upv_all.at[grp, tp]),
        (ten, ten_buf, ten_all.at[tp]),
        (tok, tok_buf, tok_all.at[tp]),
        (down, down_buf, down_all.at[grp]),
    )
    for i, (source, held, target) in enumerate(moves):
        pltpu.make_async_copy(source, held, local_in.at[i]).start()
    for i, (source, held, target) in enumerate(moves):
        pltpu.make_async_copy(source, held, local_in.at[i]).wait()
        pltpu.make_async_copy(held, target, local_out.at[i]).start()
    for i, (source, held, target) in enumerate(moves):
        pltpu.make_async_copy(held, target, local_out.at[i]).wait()

    for d in range(1, max(n1, n2) + 1):
        if d < n1:
            big.first_step(d)
        if d == 1:
            for e in range(1, n2):
                small.first_step(e)
            for i in range(1, members):
                src_tp = lax.rem(tp + i, members)
                for copy in peers(src_tp, src_tp):
                    copy.wait_recv()
            ups_q.begin()
            ups_v.begin()
        if 1 < d <= n1:
            for e in range(n2):
                small.second_step(e, d - 1)
    for chain in (downs, ups_q, ups_v):
        for d in range(1, nx):
            chain.first_step(d)
    big.finish_second()
    for chain in (downs, ups_q, ups_v):
        chain.finish_second()
    for chain in (big, small, downs, ups_q, ups_v):
        chain.drain()
    for i in range(1, members):
        for copy in peers(lax.rem(tp + i, members), tp):
            copy.wait_send()


def gather_all(tokens, tenant, down, up_q, up_v, groups, members):
    n1, n2 = factor(members)
    nx, nc = groups // 2, 2
    rows = tokens.shape[0]
    each, rank = up_q.shape[:2]
    cq, cv = up_q.shape[2] // members, up_v.shape[2] // members
    ten = jnp.broadcast_to(tenant[:, None], (rows, 128))
    up_v = up_v.reshape(each, rank, members, cv).transpose(2, 0, 1, 3)
    shape = jax.ShapeDtypeStruct
    dma = pltpu.SemaphoreType.DMA
    grid2 = (dma((nx, nc, 4)), dma((nx, nc)))
    return pl.pallas_call(
        functools.partial(exchange, (groups, members)),
        out_shape=(
            shape((members,) + tokens.shape, BF16),
            shape((members, rows, 128), jnp.int32),
            shape((groups,) + down.shape, BF16),
            shape((groups, members, each, rank, cq), BF16),
            shape((groups, members, each, rank, cv), BF16),
        ),
        in_specs=[pl.BlockSpec(memory_space=pl.ANY)] * 5,
        out_specs=(pl.BlockSpec(memory_space=pl.ANY),) * 5,
        scratch_shapes=[
            pltpu.VMEM(tokens.shape, BF16),
            pltpu.VMEM((rows, 128), jnp.int32),
            pltpu.VMEM(down.shape, BF16),
            pltpu.VMEM((each, rank, cq), BF16),
            pltpu.VMEM((each, rank, cv), BF16),
            dma((n1, n2, 4)), dma((n1, n2)),
            dma((n2, n1, 4)), dma((n2, n1)),
            *grid2, *grid2, *grid2,
            dma((members,)), dma((members,)), dma((members,)), dma((members,)), dma((members,)), dma((members,)),
            dma((5,)), dma((5,)),
        ],
        compiler_params=pltpu.CompilerParams(collective_id=0, has_side_effects=True),
    )(tokens, ten, down, up_q, up_v)


def down_kernel(members, tok, ten, down, out):
    step = pl.program_id(0)
    each = down.shape[1]

    @pl.when(step == 0)
    def _():
        out[...] = jnp.zeros_like(out)

    maps = jnp.concatenate([down[0, i] for i in range(each)], axis=1)
    part = jnp.dot(tok[...], maps, preferred_element_type=F32)
    width = down.shape[3]
    first = (step * members + lax.axis_index("tp")) * each
    for i in range(each):
        keep = ten[...] == first + i
        out[...] += jnp.where(keep, part[:, i * width:(i + 1) * width], 0.0).astype(out.dtype)


def down_project(tok, ten, down, members):
    total = tok.shape[0]
    groups = down.shape[0]
    return pl.pallas_call(
        functools.partial(down_kernel, members),
        grid=(groups,),
        out_shape=jax.ShapeDtypeStruct((total, down.shape[3]), BF16),
        in_specs=[
            pl.BlockSpec(tok.shape, lambda g: (0, 0), pipeline_mode=pl.Buffered(1)),
            pl.BlockSpec(ten.shape, lambda g: (0, 0)),
            pl.BlockSpec((1,) + down.shape[1:], lambda g: (g, 0, 0, 0)),
        ],
        out_specs=pl.BlockSpec((total, down.shape[3]), lambda g: (0, 0)),
        compiler_params=pltpu.CompilerParams(vmem_limit_bytes=60 << 20),
    )(tok, ten, down)


def finish_kernel(
    members, rank, part, ten, base_q, base_v, upq, upv, out_q, out_v,
    inbox, mine, low, wide, held_q, held_v,
    s1, r1, s2, r2, sq, rq, sv, rv, loc,
):
    grp, me = lax.axis_index("grp"), lax.axis_index("tp")
    rows = mine.shape[0]
    width = mine.shape[1]
    cols_q = base_q.shape[1]
    pair = 2 * rows
    pairs = members // 2

    barrier = pltpu.get_barrier_semaphore()
    for i in range(1, members):
        pl.semaphore_signal(barrier, inc=1, device_id=(grp, lax.rem(me + i, members)), device_id_type=MESH)
    pl.semaphore_wait(barrier, members - 1)

    def remote(src, dst, send, recv, j):
        return pltpu.make_async_remote_copy(
            src_ref=src, dst_ref=dst, send_sem=send, recv_sem=recv, device_id=(grp, j), device_id_type=MESH
        )

    def collect(j, source):
        return remote(part.at[j], inbox.at[source], s1.at[j], r1.at[source], j)

    def spread(j, source):
        return remote(mine, low.at[source], s2.at[j], r2.at[source], j)

    own = pltpu.make_async_copy(part.at[me], inbox.at[me], loc.at[0])
    own.start()
    for i in range(1, members):
        collect(lax.rem(me + i, members), me).start()
    own.wait()
    for i in range(1, members):
        j = lax.rem(me + i, members)
        collect(j, j).wait_recv()
    total = inbox[0].astype(F32)
    for i in range(1, members):
        total = total + inbox[i].astype(F32)
    mine[...] = (adapter_scale * total).astype(BF16)
    for i in range(1, members):
        collect(lax.rem(me + i, members), me).wait_send()
    for i in range(1, members):
        spread(lax.rem(me + i, members), me).start()
    own = pltpu.make_async_copy(mine, low.at[me], loc.at[0])
    own.start()
    own.wait()
    for i in range(1, members):
        j = lax.rem(me + i, members)
        spread(j, j).wait_recv()
    for i in range(1, members):
        spread(lax.rem(me + i, members), me).wait_send()

    lane = lax.broadcasted_iota(jnp.int32, (pair, width), 1)
    share = lane // rank
    count = upq.shape[0] // rank

    def home(j, source):
        columns = pl.ds(pl.multiple_of(source * cols_q, cols_q), cols_q)
        return (
            remote(held_q.at[j], out_q.at[:, columns], sq.at[j], rq.at[source], j),
            remote(held_v.at[j], out_v.at[source], sv.at[j], rv.at[source], j),
        )

    def kept():
        columns = pl.ds(pl.multiple_of(me * cols_q, cols_q), cols_q)
        return (
            pltpu.make_async_copy(held_q.at[me], out_q.at[:, columns], loc.at[0]),
            pltpu.make_async_copy(held_v.at[me], out_v.at[me], loc.at[1]),
        )

    def place(i):
        return lax.rem(me // 2 + i + 1, pairs)

    def send(i):
        for k in range(2):
            j = 2 * place(i) + k

            @pl.when(j != me)
            def _():
                for copy in home(j, me):
                    copy.start()

            @pl.when(j == me)
            def _():
                for copy in kept():
                    copy.start()

    def body(i, carry):
        p = place(i)
        at = pl.ds(pl.multiple_of(p * pair, pair), pair)
        tenant = ten[at, :]
        value = low[pl.ds(2 * p, 2)].reshape(pair, width).astype(F32)
        turned = pltpu.roll(value, rank, 1)
        parts = (jnp.where(lane < rank, value, turned), jnp.where(lane < rank, turned, value))
        for which, (base, up, held) in enumerate(((base_q, upq, held_q), (base_v, upv, held_v))):
            for c in range(count // 2):
                keep = tenant == share + 2 * c
                wide[:, c * width:(c + 1) * width] = jnp.where(keep, parts[which], 0.0).astype(BF16)
            result = base[at, :] + jnp.dot(wide[...], up[...], preferred_element_type=F32)
            held[pl.ds(2 * p, 2)] = result.astype(BF16).reshape(2, rows, result.shape[1])

        @pl.when(i > 0)
        def _():
            send(i - 1)

        return carry

    lax.fori_loop(0, pairs, body, 0)
    send(pairs - 1)
    for i in range(1, members):
        j = lax.rem(me + i, members)
        for copy in home(j, j):
            copy.wait_recv()
        for copy in home(j, me):
            copy.wait_send()
    for copy in kept():
        copy.wait()


def finish(part, ten, base_q, base_v, upq, upv, members, rank):
    total, width = part.shape
    rows = total // members
    cq, cv = base_q.shape[1], base_v.shape[1]
    dma = pltpu.SemaphoreType.DMA
    whole = pl.BlockSpec(memory_space=pltpu.VMEM)
    left = pl.BlockSpec(memory_space=pl.ANY)
    queries, values = pl.pallas_call(
        functools.partial(finish_kernel, members, rank),
        out_shape=(
            jax.ShapeDtypeStruct((rows, members * cq), BF16),
            jax.ShapeDtypeStruct((members, rows, cv), BF16),
        ),
        in_specs=[left, whole, whole, whole, whole, whole],
        out_specs=(left, left),
        scratch_shapes=[
            pltpu.VMEM((members, rows, width), BF16),
            pltpu.VMEM((rows, width), BF16),
            pltpu.VMEM((members, rows, width), BF16),
            pltpu.VMEM((2 * rows, upq.shape[0]), BF16),
            pltpu.VMEM((members, rows, cq), BF16),
            pltpu.VMEM((members, rows, cv), BF16),
            *[dma((members,))] * 8,
            dma((2,)),
        ],
        compiler_params=pltpu.CompilerParams(
            collective_id=1, has_side_effects=True, vmem_limit_bytes=58 << 20
        ),
    )(part.reshape(members, rows, width), ten, base_q, base_v, upq, upv)
    return queries, values.transpose(1, 0, 2).reshape(rows, members * cv)


def on_device(tokens, holder, choice, wq, wv, down, up_q, up_v):
    members = lax.axis_size("tp")
    groups = lax.axis_size("grp")
    each, rank, _ = up_q.shape
    mine = (holder[:, 0] * each + choice[:, 0]).astype(jnp.int32)
    tok, ten, downs, all_q, all_v = gather_all(tokens, mine, down, up_q, up_v, groups, members)
    total = members * tokens.shape[0]
    tok = tok.reshape(total, tokens.shape[1])
    ten = ten.reshape(total, 128)
    low = down_project(tok, ten, downs, members)
    base_q = jnp.dot(tok, wq, preferred_element_type=F32)
    base_v = jnp.dot(tok, wv, preferred_element_type=F32)
    depth = groups * members * each * rank
    queries, values = finish(
        low, ten, base_q, base_v, all_q.reshape(depth, -1), all_v.reshape(depth, -1), members, rank
    )
    return queries, values


def solution(mesh):
    rows = P(("grp", "tp"), None)
    blocks = P(("grp", "tp"), None, None)
    return jax.shard_map(
        on_device,
        mesh=mesh,
        in_specs=(rows, rows, rows, P(None, "tp"), P(None, "tp"), blocks, blocks, blocks),
        out_specs=(rows, rows),
        check_vma=False,
    )
```

```python
import functools

import jax
import jax.numpy as jnp
from jax import lax
from jax.experimental import pallas as pl
from jax.experimental.pallas import tpu as pltpu
from jax.sharding import PartitionSpec as P

adapter_scale = 2.0
F32 = jnp.float32
BF16 = jnp.bfloat16
MESH = pl.DeviceIdType.MESH


def factor(n):
    first = 1
    while first * first < n:
        first *= 2
    return first, n // first


class Chain:
    def __init__(self, n1, n2, a, b, place, own, send, recv, device):
        self.n1, self.n2, self.a, self.b = n1, n2, a, b
        self.place, self.own, self.send, self.recv, self.device = place, own, send, recv, device

    def copy(self, block, s, t, way, to_a, to_b):
        return pltpu.make_async_remote_copy(
            src_ref=block,
            dst_ref=self.place(s, t),
            send_sem=self.send.at[s, t, way],
            recv_sem=self.recv.at[s, t],
            device_id=self.device(to_a, to_b),
            device_id_type=MESH,
        )

    def ways(self, s, t):
        a, b = self.a, self.b
        in_line = t == b
        return (
            (in_line & (s <= a) & (a + 1 < self.n1), 0, a + 1, b),
            (in_line & (s >= a) & (a >= 1), 1, a - 1, b),
            ((t <= b) & (b + 1 < self.n2), 2, a, b + 1),
            ((t >= b) & (b >= 1), 3, a, b - 1),
        )

    def each(self, s, t, act, own):
        block = self.own if own else self.place(s, t)
        for cond, way, to_a, to_b in self.ways(s, t):
            if self.n2 == 1 and way >= 2:
                continue

            @pl.when(cond)
            def _(way=way, to_a=to_a, to_b=to_b):
                act(self.copy(block, s, t, way, to_a, to_b))

    def begin(self):
        self.each(self.a, self.b, lambda c: c.start(), True)

    def arrive(self, s, t):
        self.copy(self.place(s, t), s, t, 0, self.a, self.b).wait_recv()
        self.each(s, t, lambda c: c.start(), False)

    def first_step(self, d):
        for s, ok in ((self.a - d, self.a >= d), (self.a + d, self.a + d < self.n1)):

            @pl.when(ok)
            def _(s=s):
                self.arrive(s, self.b)

    def second_step(self, d, e):
        sides = ((self.a, None),) if d == 0 else ((self.a - d, self.a >= d), (self.a + d, self.a + d < self.n1))
        for s, ok in sides:
            for t, ok2 in ((self.b - e, self.b >= e), (self.b + e, self.b + e < self.n2)):

                @pl.when(ok2 if ok is None else ok & ok2)
                def _(s=s, t=t):
                    self.arrive(s, t)

    def finish_second(self):
        for d in range(self.n1):
            for e in range(1, self.n2):
                self.second_step(d, e)

    def drain(self):
        def body(i, carry):
            s, t = i // self.n2, i % self.n2
            self.each(s, t, lambda c: c.wait_send(), False)
            return carry

        lax.fori_loop(0, self.n1 * self.n2, body, 0)


def exchange(
    sizes, tok, ten, down, upq, upv,
    tok_all, ten_all, down_all, upq_all, upv_all,
    tok_buf, ten_buf, down_buf, upq_buf, upv_buf,
    tok_s, tok_r, down_s, down_r, q_s, q_r, v_s, v_r,
    pq_s, pq_r, pv_s, pv_r, pt_s, pt_r, local_in, local_out,
):
    groups, members = sizes
    n1, n2 = factor(members)
    nx, nc = groups // 2, 2
    grp, tp = lax.axis_index("grp"), lax.axis_index("tp")
    a, b = tp // n2, tp % n2
    gx, gc = grp // nc, grp % nc
    rows = tok.shape[0]
    cols_q = upq.shape[2] // members
    chunk = rows // tok_s.shape[0]

    barrier = pltpu.get_barrier_semaphore()
    for i in range(1, members):
        pl.semaphore_signal(barrier, inc=1, device_id=(grp, lax.rem(tp + i, members)), device_id_type=MESH)
    for i in range(1, groups):
        pl.semaphore_signal(barrier, inc=1, device_id=(lax.rem(grp + i, groups), tp), device_id_type=MESH)
    pl.semaphore_wait(barrier, members + groups - 2)

    def at_tp(first, second):
        return (grp, first * n2 + second)

    def at_grp(first, second):
        return (first * nc + second, tp)

    def token_chain(c):
        part = pl.ds(c * chunk, chunk)
        return Chain(
            n1, n2, a, b, lambda s, t: tok_all.at[s * n2 + t, part], tok.at[part], tok_s.at[c], tok_r.at[c], at_tp
        )

    def down_chain(k):
        return Chain(
            nx, nc, gx, gc, lambda s, t: down_all.at[s * nc + t, k], down.at[k], down_s.at[k], down_r.at[k], at_grp
        )

    bigs = [token_chain(c) for c in range(tok_s.shape[0])]
    downs = [down_chain(k) for k in range(down.shape[0])]
    ups_q = Chain(
        nx, nc, gx, gc, lambda s, t: upq_all.at[s * nc + t], upq_all.at[grp], q_s, q_r, at_grp
    )
    ups_v = Chain(
        nx, nc, gx, gc, lambda s, t: upv_all.at[s * nc + t], upv_all.at[grp], v_s, v_r, at_grp
    )

    def columns(ref, width, j):
        return ref.at[:, :, pl.ds(pl.multiple_of(j * width, width), width)]

    def peers(j, src_tp):
        dev = (grp, j)
        return (
            pltpu.make_async_remote_copy(
                src_ref=columns(upq, cols_q, j), dst_ref=upq_all.at[grp, src_tp],
                send_sem=pq_s.at[j], recv_sem=pq_r.at[src_tp], device_id=dev, device_id_type=MESH),
            pltpu.make_async_remote_copy(
                src_ref=upv.at[j], dst_ref=upv_all.at[grp, src_tp],
                send_sem=pv_s.at[j], recv_sem=pv_r.at[src_tp], device_id=dev, device_id_type=MESH),
            pltpu.make_async_remote_copy(
                src_ref=ten, dst_ref=ten_all.at[src_tp],
                send_sem=pt_s.at[j], recv_sem=pt_r.at[src_tp], device_id=dev, device_id_type=MESH),
        )

    for chain in bigs + downs:
        chain.begin()

    moves = (
        (columns(upq, cols_q, tp), upq_buf, upq_all.at[grp, tp]),
        (upv.at[tp], upv_buf, upv_all.at[grp, tp]),
        (ten, ten_buf, ten_all.at[tp]),
        (tok, tok_buf, tok_all.at[tp]),
        (down, down_buf, down_all.at[grp]),
    )
    for i, (source, held, target) in enumerate(moves):
        pltpu.make_async_copy(source, held, local_in.at[i]).start()
    for i, (source, held, target) in enumerate(moves):
        pltpu.make_async_copy(source, held, local_in.at[i]).wait()
        pltpu.make_async_copy(held, target, local_out.at[i]).start()
    for i, (source, held, target) in enumerate(moves):
        pltpu.make_async_copy(held, target, local_out.at[i]).wait()

    for d in range(1, n1):
        for chain in bigs:
            chain.first_step(d)
        if d == 1:
            for i in range(1, members):
                for copy in peers(lax.rem(tp + i, members), tp):
                    copy.start()
        if d == 2:
            for chain in downs:
                for e in range(1, nx):
                    chain.first_step(e)
            for i in range(1, members):
                src_tp = lax.rem(tp + i, members)
                for copy in peers(src_tp, src_tp):
                    copy.wait_recv()
            ups_q.begin()
            ups_v.begin()
    for chain in (ups_q, ups_v):
        for e in range(1, nx):
            chain.first_step(e)
    for chain in bigs + downs + [ups_q, ups_v]:
        chain.finish_second()
    for chain in bigs + downs + [ups_q, ups_v]:
        chain.drain()
    for i in range(1, members):
        for copy in peers(lax.rem(tp + i, members), tp):
            copy.wait_send()


def gather_all(tokens, tenant, down, up_q, up_v, groups, members):
    n1, n2 = factor(members)
    nx, nc = groups // 2, 2
    rows = tokens.shape[0]
    each, rank = up_q.shape[:2]
    cq, cv = up_q.shape[2] // members, up_v.shape[2] // members
    ten = jnp.broadcast_to(tenant[:, None], (rows, 128))
    up_v = up_v.reshape(each, rank, members, cv).transpose(2, 0, 1, 3)
    shape = jax.ShapeDtypeStruct
    dma = pltpu.SemaphoreType.DMA
    grid2 = (dma((nx, nc, 4)), dma((nx, nc)))
    return pl.pallas_call(
        functools.partial(exchange, (groups, members)),
        out_shape=(
            shape((members,) + tokens.shape, BF16),
            shape((members, rows, 128), jnp.int32),
            shape((groups,) + down.shape, BF16),
            shape((groups, members, each, rank, cq), BF16),
            shape((groups, members, each, rank, cv), BF16),
        ),
        in_specs=[pl.BlockSpec(memory_space=pl.ANY)] * 5,
        out_specs=(pl.BlockSpec(memory_space=pl.ANY),) * 5,
        scratch_shapes=[
            pltpu.VMEM(tokens.shape, BF16),
            pltpu.VMEM((rows, 128), jnp.int32),
            pltpu.VMEM(down.shape, BF16),
            pltpu.VMEM((each, rank, cq), BF16),
            pltpu.VMEM((each, rank, cv), BF16),
            dma((3, n1, n2, 4)), dma((3, n1, n2)),
            dma((each, nx, nc, 4)), dma((each, nx, nc)),
            *grid2, *grid2,
            dma((members,)), dma((members,)), dma((members,)), dma((members,)), dma((members,)), dma((members,)),
            dma((5,)), dma((5,)),
        ],
        compiler_params=pltpu.CompilerParams(collective_id=0, has_side_effects=True),
    )(tokens, ten, down, up_q, up_v)


def down_kernel(members, tok, ten, down, out):
    step = pl.program_id(0)
    each = down.shape[1]

    @pl.when(step == 0)
    def _():
        out[...] = jnp.zeros_like(out)

    maps = jnp.concatenate([down[0, i] for i in range(each)], axis=1)
    part = jnp.dot(tok[...], maps, preferred_element_type=F32)
    width = down.shape[3]
    first = (step * members + lax.axis_index("tp")) * each
    for i in range(each):
        keep = ten[...] == first + i
        out[...] += jnp.where(keep, part[:, i * width:(i + 1) * width], 0.0).astype(out.dtype)


def down_project(tok, ten, down, members):
    total = tok.shape[0]
    groups = down.shape[0]
    return pl.pallas_call(
        functools.partial(down_kernel, members),
        grid=(groups,),
        out_shape=jax.ShapeDtypeStruct((total, down.shape[3]), BF16),
        in_specs=[
            pl.BlockSpec(tok.shape, lambda g: (0, 0), pipeline_mode=pl.Buffered(1)),
            pl.BlockSpec(ten.shape, lambda g: (0, 0)),
            pl.BlockSpec((1,) + down.shape[1:], lambda g: (g, 0, 0, 0)),
        ],
        out_specs=pl.BlockSpec((total, down.shape[3]), lambda g: (0, 0)),
        compiler_params=pltpu.CompilerParams(vmem_limit_bytes=60 << 20),
    )(tok, ten, down)


def finish_kernel(
    members, rank, part, ten, base_q, base_v, upq, upv, out_q, out_v,
    inbox, mine, low, wide, held_q, held_v,
    s1, r1, s2, r2, sq, rq, sv, rv, loc,
):
    grp, me = lax.axis_index("grp"), lax.axis_index("tp")
    rows = mine.shape[0]
    width = mine.shape[1]
    cols_q = base_q.shape[1]
    pair = 2 * rows
    pairs = members // 2

    barrier = pltpu.get_barrier_semaphore()
    for i in range(1, members):
        pl.semaphore_signal(barrier, inc=1, device_id=(grp, lax.rem(me + i, members)), device_id_type=MESH)
    pl.semaphore_wait(barrier, members - 1)

    def remote(src, dst, send, recv, j):
        return pltpu.make_async_remote_copy(
            src_ref=src, dst_ref=dst, send_sem=send, recv_sem=recv, device_id=(grp, j), device_id_type=MESH
        )

    def collect(j, source):
        return remote(part.at[j], inbox.at[source], s1.at[j], r1.at[source], j)

    def spread(j, source):
        return remote(mine, low.at[source], s2.at[j], r2.at[source], j)

    own = pltpu.make_async_copy(part.at[me], inbox.at[me], loc.at[0])
    own.start()
    for i in range(1, members):
        collect(lax.rem(me + i, members), me).start()
    own.wait()
    for i in range(1, members):
        j = lax.rem(me + i, members)
        collect(j, j).wait_recv()
    total = inbox[0].astype(F32)
    for i in range(1, members):
        total = total + inbox[i].astype(F32)
    mine[...] = (adapter_scale * total).astype(BF16)
    for i in range(1, members):
        collect(lax.rem(me + i, members), me).wait_send()
    for i in range(1, members):
        spread(lax.rem(me + i, members), me).start()
    own = pltpu.make_async_copy(mine, low.at[me], loc.at[0])
    own.start()
    own.wait()
    for i in range(1, members):
        j = lax.rem(me + i, members)
        spread(j, j).wait_recv()
    for i in range(1, members):
        spread(lax.rem(me + i, members), me).wait_send()

    lane = lax.broadcasted_iota(jnp.int32, (pair, width), 1)
    share = lane // rank
    count = upq.shape[0] // rank

    def home(j, source):
        columns = pl.ds(pl.multiple_of(source * cols_q, cols_q), cols_q)
        return (
            remote(held_q.at[j], out_q.at[:, columns], sq.at[j], rq.at[source], j),
            remote(held_v.at[j], out_v.at[source], sv.at[j], rv.at[source], j),
        )

    def kept():
        columns = pl.ds(pl.multiple_of(me * cols_q, cols_q), cols_q)
        return (
            pltpu.make_async_copy(held_q.at[me], out_q.at[:, columns], loc.at[0]),
            pltpu.make_async_copy(held_v.at[me], out_v.at[me], loc.at[1]),
        )

    def place(i):
        return lax.rem(me // 2 + i + 1, pairs)

    def send(i):
        for k in range(2):
            j = 2 * place(i) + k

            @pl.when(j != me)
            def _():
                for copy in home(j, me):
                    copy.start()

            @pl.when(j == me)
            def _():
                for copy in kept():
                    copy.start()

    def body(i, carry):
        p = place(i)
        at = pl.ds(pl.multiple_of(p * pair, pair), pair)
        tenant = ten[at, :]
        value = low[pl.ds(2 * p, 2)].reshape(pair, width).astype(F32)
        turned = pltpu.roll(value, rank, 1)
        parts = (jnp.where(lane < rank, value, turned), jnp.where(lane < rank, turned, value))
        for which, (base, up, held) in enumerate(((base_q, upq, held_q), (base_v, upv, held_v))):
            for c in range(count // 2):
                keep = tenant == share + 2 * c
                wide[:, c * width:(c + 1) * width] = jnp.where(keep, parts[which], 0.0).astype(BF16)
            result = base[at, :] + jnp.dot(wide[...], up[...], preferred_element_type=F32)
            held[pl.ds(2 * p, 2)] = result.astype(BF16).reshape(2, rows, result.shape[1])

        @pl.when(i > 0)
        def _():
            send(i - 1)

        return carry

    lax.fori_loop(0, pairs, body, 0)
    send(pairs - 1)
    for i in range(1, members):
        j = lax.rem(me + i, members)
        for copy in home(j, j):
            copy.wait_recv()
        for copy in home(j, me):
            copy.wait_send()
    for copy in kept():
        copy.wait()


def finish(part, ten, base_q, base_v, upq, upv, members, rank):
    total, width = part.shape
    rows = total // members
    cq, cv = base_q.shape[1], base_v.shape[1]
    dma = pltpu.SemaphoreType.DMA
    whole = pl.BlockSpec(memory_space=pltpu.VMEM)
    left = pl.BlockSpec(memory_space=pl.ANY)
    queries, values = pl.pallas_call(
        functools.partial(finish_kernel, members, rank),
        out_shape=(
            jax.ShapeDtypeStruct((rows, members * cq), BF16),
            jax.ShapeDtypeStruct((members, rows, cv), BF16),
        ),
        in_specs=[left, whole, whole, whole, whole, whole],
        out_specs=(left, left),
        scratch_shapes=[
            pltpu.VMEM((members, rows, width), BF16),
            pltpu.VMEM((rows, width), BF16),
            pltpu.VMEM((members, rows, width), BF16),
            pltpu.VMEM((2 * rows, upq.shape[0]), BF16),
            pltpu.VMEM((members, rows, cq), BF16),
            pltpu.VMEM((members, rows, cv), BF16),
            *[dma((members,))] * 8,
            dma((2,)),
        ],
        compiler_params=pltpu.CompilerParams(
            collective_id=1, has_side_effects=True, vmem_limit_bytes=58 << 20
        ),
    )(part.reshape(members, rows, width), ten, base_q, base_v, upq, upv)
    return queries, values.transpose(1, 0, 2).reshape(rows, members * cv)


def on_device(tokens, holder, choice, wq, wv, down, up_q, up_v):
    members = lax.axis_size("tp")
    groups = lax.axis_size("grp")
    each, rank, _ = up_q.shape
    mine = (holder[:, 0] * each + choice[:, 0]).astype(jnp.int32)
    tok, ten, downs, all_q, all_v = gather_all(tokens, mine, down, up_q, up_v, groups, members)
    total = members * tokens.shape[0]
    tok = tok.reshape(total, tokens.shape[1])
    ten = ten.reshape(total, 128)
    low = down_project(tok, ten, downs, members)
    base_q = jnp.dot(tok, wq, preferred_element_type=F32)
    base_v = jnp.dot(tok, wv, preferred_element_type=F32)
    depth = groups * members * each * rank
    queries, values = finish(
        low, ten, base_q, base_v, all_q.reshape(depth, -1), all_v.reshape(depth, -1), members, rank
    )
    return queries, values


def solution(mesh):
    rows = P(("grp", "tp"), None)
    blocks = P(("grp", "tp"), None, None)
    return jax.shard_map(
        on_device,
        mesh=mesh,
        in_specs=(rows, rows, rows, P(None, "tp"), P(None, "tp"), blocks, blocks, blocks),
        out_specs=(rows, rows),
        check_vma=False,
    )
```
